512 devices in a mesh: fsdp: 64 (over y_lo, z, core), tp: 8 (over x, y_hi).
Axes of the slice: x: 4, y: 8 (y_hi: 2, y_lo: 4; y = y_hi * 4 + y_lo), z: 8, core: 2. Of those that a mesh axis runs over, the one named last changes fastest.
Arguments:
- images: bfloat16 [64, 256, 6144], P('fsdp', None, 'tp'), may hold values from -6 to 6
- keep_index: int32 [64, 64], P('fsdp'), may hold values from 0 to 255, as said below
- teacher_weight: float32 [6144, 3072], P('fsdp', 'tp'), may hold values from -0.078125 to 0.078125
- student_weight: float32 [6144, 3072], P('fsdp', 'tp'), may hold values from -0.078125 to 0.078125
Outputs:
- teacher_next: float32 [6144, 3072], P('fsdp', 'tp')
- student_grad: float32 [6144, 3072], P('fsdp', 'tp')
The draws below stay inside these ranges and needn't reach their ends.
Inputs may be any that keep to these rules, and one draw needn't show every extreme that they name: `keep_index`: each image's 64 indices are distinct and increasing.
All inputs are finite; a program needn't handle non-finite values.
Results may differ from the reference program's by a relative error of at most 0.0048.
Values may be sent and summed in bfloat16 or wider, within the bound.
No kernel may reach another device: no remote copies, remote signals or barrier semaphores. Data moves between devices by JAX's collectives and lax.ppermute only.
A program may use at most 64 MiB of HBM per device.

```python
import math
import jax
import jax.numpy as jnp
from jax import lax

D = 6144
PATCHES = 256
KEEP = 64
IMAGES = 64
PROJ = 3072


def draw_keep_index(key, part):
    streams = jax.random.split(jax.random.fold_in(key, 7), IMAGES)

    def one_image(stream):
        order = jax.random.permutation(stream, PATCHES)
        return jnp.sort(order[:KEEP]).astype(jnp.int32)
    return jax.vmap(one_image)(streams)


def steps_of(own_key, dims, shards, smallest, largest):
    gain = 1.0
    for position, shards_of in shards:
        heights = jax.random.uniform(jax.random.fold_in(jax.random.fold_in(own_key, 6), position), (shards_of,), jnp.float32, smallest / len(shards), largest / len(shards))
        gain = gain * jnp.repeat(jnp.exp(heights), dims[position] // shards_of).reshape((-1,) + (1,) * (len(dims) - 1 - position))
    return gain


def scatter_about(own_key, extent, scale, most, shards=(), dtype=jnp.bfloat16):
    result = jax.random.normal(own_key, extent, jnp.float32) * scale
    if len(shards) > 0:
        result = steps_of(own_key, extent, shards, -0.22, 0.18) * result
    return jnp.clip(result, min=-most, max=most).astype(dtype)


def setup_inputs(seed: int = 0) -> dict:
    key_list = jax.random.split(jax.random.key(seed), 5)
    return {
        "images": scatter_about(key_list[0], (IMAGES, PATCHES, D), 1.0, 6.0, ((0, 64), (2, 8))),
        "keep_index": draw_keep_index(jax.random.fold_in(key_list[4], 71), 0),
        "teacher_weight": scatter_about(key_list[2], (D, PROJ), D ** -0.5, 0.078125, ((0, 64), (1, 8)), jnp.float32),
        "student_weight": scatter_about(key_list[3], (D, PROJ), D ** -0.5, 0.078125, ((0, 64), (1, 8)), jnp.float32),
    }


def layer_norm(values):
    floats = values.astype(jnp.float32)
    centre = lax.optimization_barrier(jnp.mean(floats, axis=-1, keepdims=True))
    centred = floats - centre
    spread = lax.optimization_barrier(jnp.mean(centred * centred, axis=-1, keepdims=True))
    return (centred * lax.rsqrt(spread + 1e-06)).astype(jnp.bfloat16)

def pick_rows(table, index):
    return jax.vmap(lambda block, rows: block[rows])(table, index)

def reference(images, keep_index, teacher_weight, student_weight):
    teacher_next = 0.999 * teacher_weight + (1.0 - 0.999) * student_weight
    teacher_panel = teacher_next.astype(jnp.bfloat16)
    student_panel = student_weight.astype(jnp.bfloat16)
    normed = layer_norm(images)
    teacher_out = jnp.dot(normed.reshape(-1, D), teacher_panel, preferred_element_type=jnp.float32)
    teacher_out = teacher_out.reshape(IMAGES, PATCHES, -1)
    centre = lax.optimization_barrier(jnp.mean(teacher_out, axis=1, keepdims=True))
    centred = teacher_out - centre
    spread = lax.optimization_barrier(jnp.mean(centred * centred, axis=1, keepdims=True))
    target = centred * lax.rsqrt(spread + 1e-05)
    picked = pick_rows(normed, keep_index).reshape(-1, D)
    target_kept = pick_rows(target, keep_index).reshape(picked.shape[0], -1)
    student_out = jnp.dot(picked, student_panel, preferred_element_type=jnp.float32)
    error = ((student_out - target_kept) * (1.0 / math.sqrt(IMAGES * KEEP))).astype(jnp.bfloat16)
    student_grad = jnp.dot(picked.T, error, preferred_element_type=jnp.float32)
    return (teacher_next, student_grad)
```

```python
import math

import jax
import jax.numpy as jnp
from jax import lax
from jax.experimental import pallas as pl
from jax.experimental.pallas import tpu as pltpu
from jax.sharding import Mesh
from jax.sharding import PartitionSpec as P

D = 6144
Y, Z, C, X, H = 4, 8, 2, 4, 2
BF, F32 = jnp.bfloat16, jnp.float32
MB = 1024 * 1024


def normalise_kernel(image_ref, centre_ref, scale_ref, select_ref, normed_ref, picked_ref):
    values = image_ref[0].astype(F32)
    normed = ((values - centre_ref[...]) * scale_ref[...]).astype(BF)
    normed_ref[0] = normed
    picked_ref[0] = jnp.dot(select_ref[...], normed, preferred_element_type=F32).astype(BF)


def normalise(chunks, centre, scale, select):
    n, patches, width = chunks.shape
    keep = select.shape[0]
    small = pl.BlockSpec((patches, 1), lambda k: (0, 0))
    return pl.pallas_call(
        normalise_kernel,
        grid=(n,),
        in_specs=[
            pl.BlockSpec((1, patches, width), lambda k: (k, 0, 0)),
            small,
            small,
            pl.BlockSpec((keep, patches), lambda k: (0, 0)),
        ],
        out_specs=[
            pl.BlockSpec((1, patches, width), lambda k: (k, 0, 0)),
            pl.BlockSpec((1, keep, width), lambda k: (k, 0, 0)),
        ],
        out_shape=[
            jax.ShapeDtypeStruct((n, patches, width), BF),
            jax.ShapeDtypeStruct((n, keep, width), BF),
        ],
        compiler_params=pltpu.CompilerParams(vmem_limit_bytes=24 * MB),
        cost_estimate=pl.CostEstimate(
            flops=2 * n * keep * patches * width, bytes_accessed=2 * n * width * (2 * patches + keep), transcendentals=0
        ),
    )(chunks, centre, scale, select)


def error_kernel(factor, normed_ref, picked_ref, panel_ref, error_ref, teacher_acc, kept_acc):
    step = pl.program_id(0)
    columns = error_ref.shape[1]

    @pl.when(step == 0)
    def _():
        teacher_acc[...] = jnp.zeros_like(teacher_acc)
        kept_acc[...] = jnp.zeros_like(kept_acc)

    panel = panel_ref[:, 0].reshape(-1, 2 * columns)
    teacher_acc[...] += jnp.dot(normed_ref[0], panel[:, :columns], preferred_element_type=F32)
    kept_acc[...] += jnp.dot(picked_ref[0], panel, preferred_element_type=F32)

    @pl.when(step == pl.num_programs(0) - 1)
    def _():
        teacher = teacher_acc[...]
        centre = jnp.mean(teacher, axis=0, keepdims=True)
        centred = teacher - centre
        spread = jnp.mean(centred * centred, axis=0, keepdims=True)
        target = (kept_acc[:, :columns] - centre) * lax.rsqrt(spread + 1e-05)
        error_ref[...] = ((kept_acc[:, columns:] - target) * factor).astype(BF)


def make_error(normed, picked, panels, factor):
    n, patches, width = normed.shape
    keep = picked.shape[1]
    blocks, _, rows, both = panels.shape
    columns = both // 2

    def body(*refs):
        error_kernel(factor, *refs)

    return pl.pallas_call(
        body,
        grid=(n,),
        in_specs=[
            pl.BlockSpec((1, patches, width), lambda k: (k, 0, 0)),
            pl.BlockSpec((1, keep, width), lambda k: (k, 0, 0)),
            pl.BlockSpec((blocks, 1, rows, both), lambda k: (0, k, 0, 0)),
        ],
        out_specs=pl.BlockSpec((keep, columns), lambda k: (0, 0)),
        out_shape=jax.ShapeDtypeStruct((keep, columns), BF),
        scratch_shapes=[pltpu.VMEM((patches, columns), F32), pltpu.VMEM((keep, both), F32)],
        compiler_params=pltpu.CompilerParams(vmem_limit_bytes=56 * MB),
        cost_estimate=pl.CostEstimate(
            flops=2 * n * width * (patches * columns + keep * both),
            bytes_accessed=2 * n * width * (patches + keep + both),
            transcendentals=columns,
        ),
    )(normed, picked, panels)


def spread_to_all(values, axes, size):
    return lax.all_to_all(jnp.broadcast_to(values[None], (size, *values.shape)), axes, split_axis=0, concat_axis=0)


def shards(images, keep_index, teacher_weight, student_weight):
    patches, slice_width = images.shape[1:]
    keep_count = keep_index.shape[1]
    rows, columns = teacher_weight.shape
    image = images[0]

    teacher_next = 0.999 * teacher_weight + (1.0 - 0.999) * student_weight
    panel = jnp.concatenate([teacher_next, student_weight], axis=1).astype(BF)
    other = lax.ppermute(image, "yh", [(0, 1), (1, 0)])
    panels = lax.all_gather(panel, "yl", axis=0, tiled=True)
    panels, other = lax.optimization_barrier((panels, other))
    panels = lax.all_gather(panels, ("z", "c"), axis=0, tiled=True).reshape(Z * C, Y, rows, 2 * columns)

    pair = jnp.where(
        lax.axis_index("yh") == 0,
        jnp.concatenate([image, other], axis=1),
        jnp.concatenate([other, image], axis=1),
    )
    whole = lax.all_gather(pair, "x", axis=0, tiled=False)

    floats = image.astype(F32)
    own_mean = jnp.mean(floats, axis=1)
    own_moment = jnp.sum(jnp.square(floats - own_mean[:, None]), axis=1)
    parts = spread_to_all(jnp.stack([own_mean, own_moment]), ("x", "yh"), X * H)
    centre = jnp.mean(parts[:, 0], axis=0)
    moment = jnp.sum(parts[:, 1], axis=0) + slice_width * jnp.sum(jnp.square(parts[:, 0] - centre), axis=0)
    scale = lax.rsqrt(moment / D + 1e-06)
    centre, scale = centre[:, None], scale[:, None]

    select = (keep_index[0][:, None] == lax.broadcasted_iota(jnp.int32, (keep_count, patches), 1)).astype(BF)

    _, picked_pair = normalise(pair[None], centre, scale, select)
    pieces = picked_pair[0].reshape(keep_count, Z * C, rows).transpose(1, 0, 2)
    pieces = lax.all_to_all(pieces, ("z", "c"), split_axis=0, concat_axis=0)
    owned = spread_to_all(pieces, "x", X)
    owned = owned.reshape(Y, Z * C * keep_count, rows).transpose(0, 2, 1).reshape(Y * rows, Z * C * keep_count)

    normed, picked = normalise(whole, centre, scale, select)
    total_kept = keep_count * Y * Z * C
    error = make_error(normed, picked, panels, 1.0 / math.sqrt(total_kept))
    errors = lax.all_gather(error, ("z", "c"), axis=0, tiled=True)
    partial = jnp.dot(owned, errors, preferred_element_type=F32).astype(BF).reshape(Y, rows, columns)
    partial = lax.all_to_all(partial, "yl", split_axis=0, concat_axis=0)
    student_grad = jnp.sum(partial.astype(F32), axis=0)
    return (teacher_next, student_grad)


def solution(mesh):
    fine = Mesh(mesh.devices.reshape(Y, Z, C, X, H), ("yl", "z", "c", "x", "yh"))
    rows, cols = ("yl", "z", "c"), ("x", "yh")
    return jax.shard_map(
        shards,
        mesh=fine,
        in_specs=(P(rows, None, cols), P(rows, None), P(rows, cols), P(rows, cols)),
        out_specs=(P(rows, cols), P(rows, cols)),
        check_vma=False,
    )
```

```python
import math

import jax
import jax.numpy as jnp
from jax import lax
from jax.experimental import pallas as pl
from jax.experimental.pallas import tpu as pltpu
from jax.sharding import Mesh
from jax.sharding import PartitionSpec as P

D = 6144
Y, Z, C, X, H = 4, 8, 2, 4, 2
BF, F32 = jnp.bfloat16, jnp.float32
MB = 1024 * 1024


def normalise_kernel(image_ref, centre_ref, scale_ref, select_ref, normed_ref, picked_ref):
    values = image_ref[0].astype(F32)
    normed = ((values - centre_ref[...]) * scale_ref[...]).astype(BF)
    normed_ref[0] = normed
    picked_ref[0] = jnp.dot(select_ref[...], normed, preferred_element_type=F32).astype(BF)


def normalise(chunks, centre, scale, select):
    n, patches, width = chunks.shape
    keep = select.shape[0]
    small = pl.BlockSpec((patches, 1), lambda k: (0, 0))
    return pl.pallas_call(
        normalise_kernel,
        grid=(n,),
        in_specs=[
            pl.BlockSpec((1, patches, width), lambda k: (k, 0, 0)),
            small,
            small,
            pl.BlockSpec((keep, patches), lambda k: (0, 0)),
        ],
        out_specs=[
            pl.BlockSpec((1, patches, width), lambda k: (k, 0, 0)),
            pl.BlockSpec((1, keep, width), lambda k: (k, 0, 0)),
        ],
        out_shape=[
            jax.ShapeDtypeStruct((n, patches, width), BF),
            jax.ShapeDtypeStruct((n, keep, width), BF),
        ],
        compiler_params=pltpu.CompilerParams(vmem_limit_bytes=24 * MB),
        cost_estimate=pl.CostEstimate(
            flops=2 * n * keep * patches * width, bytes_accessed=2 * n * width * (2 * patches + keep), transcendentals=0
        ),
    )(chunks, centre, scale, select)


def error_kernel(factor, first_ref, *refs):
    n = pl.num_programs(0)
    count = (len(refs) - 4) // 2
    normed_refs, picked_refs = refs[:count], refs[count : 2 * count]
    panel_ref, error_ref, teacher_acc, kept_acc = refs[2 * count :]
    step = pl.program_id(0)
    columns = error_ref.shape[1]
    panel = panel_ref[:, 0].reshape(-1, 2 * columns)
    for k in range(count):

        @pl.when(step == k)
        def _(k=k):
            teacher = jnp.dot(normed_refs[k][0], panel[:, :columns], preferred_element_type=F32)
            kept = jnp.dot(picked_refs[k][0], panel, preferred_element_type=F32)
            teacher_acc[...] = teacher if k == 0 else teacher_acc[...] + teacher
            kept_acc[...] = kept if k == 0 else kept_acc[...] + kept

    @pl.when(step == n - 1)
    def _():
        teacher = teacher_acc[...]
        centre = jnp.mean(teacher, axis=0, keepdims=True)
        centred = teacher - centre
        spread = jnp.mean(centred * centred, axis=0, keepdims=True)
        target = (kept_acc[:, :columns] - centre) * lax.rsqrt(spread + 1e-05)
        error_ref[...] = ((kept_acc[:, columns:] - target) * factor).astype(BF)


def make_error(normed, picked, panels, first, factor):
    n = len(normed)
    _, patches, width = normed[0].shape
    keep = picked[0].shape[1]
    blocks, _, rows, both = panels.shape
    columns = both // 2

    def body(*refs):
        error_kernel(factor, *refs)

    return pl.pallas_call(
        body,
        grid_spec=pltpu.PrefetchScalarGridSpec(
            num_scalar_prefetch=1,
            grid=(n,),
            in_specs=[pl.BlockSpec((1, patches, width), lambda k, first: (0, 0, 0))] * n
            + [pl.BlockSpec((1, keep, width), lambda k, first: (0, 0, 0))] * n
            + [pl.BlockSpec((blocks, 1, rows, both), lambda k, first: (0, lax.rem(first[0] + n - k, n), 0, 0))],
            out_specs=pl.BlockSpec((keep, columns), lambda k, first: (0, 0)),
            scratch_shapes=[pltpu.VMEM((patches, columns), F32), pltpu.VMEM((keep, both), F32)],
        ),
        out_shape=jax.ShapeDtypeStruct((keep, columns), BF),
        compiler_params=pltpu.CompilerParams(vmem_limit_bytes=56 * MB),
        cost_estimate=pl.CostEstimate(
            flops=2 * n * width * (patches * columns + keep * both),
            bytes_accessed=2 * n * width * (patches + keep + both),
            transcendentals=columns,
        ),
    )(first, *normed, *picked, panels)


def spread_to_all(values, axes, size):
    return lax.all_to_all(jnp.broadcast_to(values[None], (size, *values.shape)), axes, split_axis=0, concat_axis=0)


def shards(images, keep_index, teacher_weight, student_weight):
    patches, slice_width = images.shape[1:]
    keep_count = keep_index.shape[1]
    rows, columns = teacher_weight.shape
    image = images[0]

    teacher_next = 0.999 * teacher_weight + (1.0 - 0.999) * student_weight
    panel = jnp.concatenate([teacher_next, student_weight], axis=1).astype(BF)
    panels = lax.all_gather(panel, "yl", axis=0, tiled=True)
    panels, image = lax.optimization_barrier((panels, image))
    other = lax.ppermute(image, "yh", [(0, 1), (1, 0)])
    panels = lax.all_gather(panels, ("z", "c"), axis=0, tiled=True).reshape(Z * C, Y, rows, 2 * columns)

    pair = jnp.where(
        lax.axis_index("yh") == 0,
        jnp.concatenate([image, other], axis=1),
        jnp.concatenate([other, image], axis=1),
    )
    arrived = [lax.ppermute(pair, "x", [(i, (i + s) % X) for i in range(X)]) for s in range(1, X)]

    floats = image.astype(F32)
    own_mean = jnp.mean(floats, axis=1)
    own_moment = jnp.sum(jnp.square(floats - own_mean[:, None]), axis=1)
    parts = spread_to_all(jnp.stack([own_mean, own_moment]), ("x", "yh"), X * H)
    centre = jnp.mean(parts[:, 0], axis=0)
    moment = jnp.sum(parts[:, 1], axis=0) + slice_width * jnp.sum(jnp.square(parts[:, 0] - centre), axis=0)
    scale = lax.rsqrt(moment / D + 1e-06)
    centre, scale = centre[:, None], scale[:, None]

    select = (keep_index[0][:, None] == lax.broadcasted_iota(jnp.int32, (keep_count, patches), 1)).astype(BF)

    halves = [normalise(pair[None], centre, scale, select)]
    pieces = halves[0][1][0].reshape(keep_count, Z * C, rows).transpose(1, 0, 2)
    pieces = lax.all_to_all(pieces, ("z", "c"), split_axis=0, concat_axis=0)
    owned = spread_to_all(pieces, "x", X)
    owned = owned.reshape(Y, Z * C * keep_count, rows).transpose(0, 2, 1).reshape(Y * rows, Z * C * keep_count)

    halves += [normalise(chunk[None], centre, scale, select) for chunk in arrived]
    normed, picked = zip(*halves)
    first = lax.axis_index("x").reshape(1)
    total_kept = keep_count * Y * Z * C
    error = make_error(normed, picked, panels, first, 1.0 / math.sqrt(total_kept))
    errors = lax.all_gather(error, ("z", "c"), axis=0, tiled=True)
    partial = jnp.dot(owned, errors, preferred_element_type=F32).astype(BF).reshape(Y, rows, columns)
    partial = lax.all_to_all(partial, "yl", split_axis=0, concat_axis=0)
    student_grad = jnp.sum(partial.astype(F32), axis=0)
    return (teacher_next, student_grad)


def solution(mesh):
    fine = Mesh(mesh.devices.reshape(Y, Z, C, X, H), ("yl", "z", "c", "x", "yh"))
    rows, cols = ("yl", "z", "c"), ("x", "yh")
    return jax.shard_map(
        shards,
        mesh=fine,
        in_specs=(P(rows, None, cols), P(rows, None), P(rows, cols), P(rows, cols)),
        out_specs=(P(rows, cols), P(rows, cols)),
        check_vma=False,
    )
```

```python
import math

import jax
import jax.numpy as jnp
from jax import lax
from jax.experimental import pallas as pl
from jax.experimental.pallas import tpu as pltpu
from jax.sharding import Mesh
from jax.sharding import PartitionSpec as P

D = 6144
Y, Z, C, X, H = 4, 8, 2, 4, 2
BF, F32 = jnp.bfloat16, jnp.float32
MB = 1024 * 1024


def normalise_kernel(image_ref, centre_ref, scale_ref, select_ref, normed_ref):
    patches = image_ref.shape[0]
    normed = ((image_ref[...].astype(F32) - centre_ref[...]) * scale_ref[...]).astype(BF)
    normed_ref[:patches] = normed
    normed_ref[patches:] = jnp.dot(select_ref[...], normed, preferred_element_type=F32).astype(BF)


def normalise(chunk, centre, scale, select):
    patches, width = chunk.shape
    keep = select.shape[0]
    return pl.pallas_call(
        normalise_kernel,
        out_shape=jax.ShapeDtypeStruct((patches + keep, width), BF),
        compiler_params=pltpu.CompilerParams(vmem_limit_bytes=16 * MB),
        cost_estimate=pl.CostEstimate(
            flops=2 * keep * patches * width, bytes_accessed=2 * width * (2 * patches + keep), transcendentals=0
        ),
    )(chunk, centre, scale, select)


def error_kernel(factor, patches, where_ref, *refs):
    n = pl.num_programs(0)
    normed_refs, block_refs = refs[:Y], refs[Y:-4]
    error_ref, panel_ref, teacher_acc, student_acc = refs[-4:]
    step = pl.program_id(0)
    columns = error_ref.shape[1]
    z, c = where_ref[1], where_ref[2]
    for ref, offsets, core in block_refs_of(block_refs, c):
        for slot, offset in enumerate(offsets):
            panel_ref[lax.rem(z + Z + offset, Z) * C + core] = ref[slot, 0]
    panel = panel_ref[...].reshape(-1, 2 * columns)
    for k in range(Y):

        @pl.when(step == k)
        def _(k=k):
            teacher = jnp.dot(normed_refs[k][...], panel[:, :columns], preferred_element_type=F32)
            student = jnp.dot(normed_refs[k][patches:], panel[:, columns:], preferred_element_type=F32)
            teacher_acc[...] = teacher if k == 0 else teacher_acc[...] + teacher
            student_acc[...] = student if k == 0 else student_acc[...] + student

    @pl.when(step == n - 1)
    def _():
        teacher = teacher_acc[:patches]
        centre = jnp.mean(teacher, axis=0, keepdims=True)
        centred = teacher - centre
        spread = jnp.mean(centred * centred, axis=0, keepdims=True)
        target = (teacher_acc[patches:] - centre) * lax.rsqrt(spread + 1e-05)
        error_ref[...] = ((student_acc[...] - target) * factor).astype(BF)


NEAR, FAR = (0, -1, 1), (-2, 2, -3, 3, 4)


def block_refs_of(refs, c):
    return zip(refs, (NEAR, NEAR, FAR, FAR), (c, 1 - c, c, 1 - c))


def make_error(normed, patches, where, blocks, factor):
    n = len(normed)
    rows_in, width = normed[0].shape
    keep = rows_in - patches
    rows, both = blocks[0].shape[2:]
    columns = both // 2

    def body(*refs):
        error_kernel(factor, patches, *refs)

    return pl.pallas_call(
        body,
        grid_spec=pltpu.PrefetchScalarGridSpec(
            num_scalar_prefetch=1,
            grid=(n,),
            in_specs=[pl.BlockSpec((rows_in, width), lambda k, where: (0, 0))] * n
            + [
                pl.BlockSpec((len(b), 1, rows, both), lambda k, where: (0, lax.rem(where[0] + n - k, n), 0, 0))
                for b in blocks
            ],
            out_specs=pl.BlockSpec((keep, columns), lambda k, where: (0, 0)),
            scratch_shapes=[
                pltpu.VMEM((Z * C, rows, both), BF),
                pltpu.VMEM((rows_in, columns), F32),
                pltpu.VMEM((keep, columns), F32),
            ],
        ),
        out_shape=jax.ShapeDtypeStruct((keep, columns), BF),
        compiler_params=pltpu.CompilerParams(vmem_limit_bytes=40 * MB),
        cost_estimate=pl.CostEstimate(
            flops=2 * n * width * (rows_in + keep) * columns,
            bytes_accessed=2 * n * width * (rows_in + both),
            transcendentals=columns,
        ),
    )(where, *normed, *blocks)


def ring(size, step):
    return [(i, (i + step) % size) for i in range(size)]


def both_ways(up, down):
    return lax.ppermute(up, "z", ring(Z, 1)), lax.ppermute(down, "z", ring(Z, -1))


def spread_to_all(values, axes, size):
    return lax.all_to_all(jnp.broadcast_to(values[None], (size, *values.shape)), axes, split_axis=0, concat_axis=0)


def shards(images, keep_index, teacher_weight, student_weight):
    patches, slice_width = images.shape[1:]
    keep_count = keep_index.shape[1]
    rows, columns = teacher_weight.shape
    image = images[0]

    teacher_next = 0.999 * teacher_weight + (1.0 - 0.999) * student_weight
    panel = jnp.concatenate([teacher_next, student_weight], axis=1).astype(BF)
    panels = lax.all_gather(panel, "yl", axis=0, tiled=True)
    panels, image = lax.optimization_barrier((panels, image))
    own = panels.reshape(Y, rows, 2 * columns)
    up1, down1 = both_ways(own, own)
    other = lax.ppermute(image, "yh", ring(H, 1))
    up1, down1, other = lax.optimization_barrier((up1, down1, other))
    near = jnp.stack([own, up1, down1])
    near_other = lax.ppermute(near, "c", ring(C, 1))
    up2, down2 = both_ways(up1, down1)

    pair = jnp.where(
        lax.axis_index("yh") == 0,
        jnp.concatenate([image, other], axis=1),
        jnp.concatenate([other, image], axis=1),
    )
    arrived = [lax.ppermute(pair, "x", ring(X, step)) for step in range(1, X)]

    floats = image.astype(F32)
    own_mean = jnp.mean(floats, axis=1)
    own_moment = jnp.sum(jnp.square(floats - own_mean[:, None]), axis=1)
    parts = spread_to_all(jnp.stack([own_mean, own_moment]), ("x", "yh"), X * H)
    up2, down2, parts, pair, near_other = lax.optimization_barrier((up2, down2, parts, pair, near_other))
    up3, down3 = both_ways(up2, down2)
    centre = jnp.mean(parts[:, 0], axis=0)
    moment = jnp.sum(parts[:, 1], axis=0) + slice_width * jnp.sum(jnp.square(parts[:, 0] - centre), axis=0)
    scale = lax.rsqrt(moment / D + 1e-06)
    centre, scale = centre[:, None], scale[:, None]

    select = (keep_index[0][:, None] == lax.broadcasted_iota(jnp.int32, (keep_count, patches), 1)).astype(BF)

    normed = [normalise(pair, centre, scale, select)]
    pieces = normed[0][patches:].reshape(keep_count, Z * C, rows).transpose(1, 0, 2)
    pieces = lax.all_to_all(pieces, ("z", "c"), split_axis=0, concat_axis=0)
    up3, down3, pieces, arrived = lax.optimization_barrier((up3, down3, pieces, arrived))
    last_up, last_down = both_ways(up3[..., :columns], down3[..., columns:])
    far = jnp.stack([up2, down2, up3, down3, jnp.concatenate([last_up, last_down], axis=-1)])
    owned = spread_to_all(pieces, "x", X)
    owned = owned.reshape(Y, Z * C * keep_count, rows).transpose(0, 2, 1).reshape(Y * rows, Z * C * keep_count)

    normed += [normalise(chunk, centre, scale, select) for chunk in arrived]
    blocks = near, near_other, far, lax.ppermute(far, "c", ring(C, 1))
    where = jnp.stack([lax.axis_index("x"), lax.axis_index("z"), lax.axis_index("c")])
    total_kept = keep_count * Y * Z * C
    error = make_error(normed, patches, where, blocks, 1.0 / math.sqrt(total_kept))
    errors = lax.all_gather(error, ("z", "c"), axis=0, tiled=True)
    partial = jnp.dot(owned, errors, preferred_element_type=F32).astype(BF).reshape(Y, rows, columns)
    partial = lax.all_to_all(partial, "yl", split_axis=0, concat_axis=0)
    student_grad = jnp.sum(partial.astype(F32), axis=0)
    return (teacher_next, student_grad)


def solution(mesh):
    fine = Mesh(mesh.devices.reshape(Y, Z, C, X, H), ("yl", "z", "c", "x", "yh"))
    rows, cols = ("yl", "z", "c"), ("x", "yh")
    return jax.shard_map(
        shards,
        mesh=fine,
        in_specs=(P(rows, None, cols), P(rows, None), P(rows, cols), P(rows, cols)),
        out_specs=(P(rows, cols), P(rows, cols)),
        check_vma=False,
    )
```

```python
import math

import jax
import jax.numpy as jnp
from jax import lax
from jax.experimental import pallas as pl
from jax.experimental.pallas import tpu as pltpu
from jax.sharding import Mesh
from jax.sharding import PartitionSpec as P

D = 6144
Y, Z, C, X, H = 4, 8, 2, 4, 2
BF, F32 = jnp.bfloat16, jnp.float32
MB = 1024 * 1024


def normalise_kernel(image_ref, centre_ref, scale_ref, select_ref, normed_ref):
    patches = image_ref.shape[0]
    normed = ((image_ref[...].astype(F32) - centre_ref[...]) * scale_ref[...]).astype(BF)
    normed_ref[:patches] = normed
    normed_ref[patches:] = jnp.dot(select_ref[...], normed, preferred_element_type=F32).astype(BF)


def normalise(chunk, centre, scale, select):
    patches, width = chunk.shape
    keep = select.shape[0]
    return pl.pallas_call(
        normalise_kernel,
        out_shape=jax.ShapeDtypeStruct((patches + keep, width), BF),
        compiler_params=pltpu.CompilerParams(vmem_limit_bytes=16 * MB),
        cost_estimate=pl.CostEstimate(
            flops=2 * keep * patches * width, bytes_accessed=2 * width * (2 * patches + keep), transcendentals=0
        ),
    )(chunk, centre, scale, select)


def error_kernel(factor, patches, x_ref, *refs):
    n = pl.num_programs(0)
    normed_refs = refs[:Y]
    panel_ref, error_ref, teacher_acc, student_acc = refs[Y:]
    step = pl.program_id(0)
    columns = error_ref.shape[1]
    panel = panel_ref[:, 0].reshape(-1, 2 * columns)
    for k in range(Y):

        @pl.when(step == k)
        def _(k=k):
            teacher = jnp.dot(normed_refs[k][...], panel[:, :columns], preferred_element_type=F32)
            student = jnp.dot(normed_refs[k][patches:], panel[:, columns:], preferred_element_type=F32)
            teacher_acc[...] = teacher if k == 0 else teacher_acc[...] + teacher
            student_acc[...] = student if k == 0 else student_acc[...] + student

    @pl.when(step == n - 1)
    def _():
        teacher = teacher_acc[:patches]
        centre = jnp.mean(teacher, axis=0, keepdims=True)
        centred = teacher - centre
        spread = jnp.mean(centred * centred, axis=0, keepdims=True)
        target = (teacher_acc[patches:] - centre) * lax.rsqrt(spread + 1e-05)
        error_ref[...] = ((student_acc[...] - target) * factor).astype(BF)


def make_error(normed, patches, x, panels, factor):
    n = len(normed)
    rows_in, width = normed[0].shape
    keep = rows_in - patches
    blocks, _, rows, both = panels.shape
    columns = both // 2

    def body(*refs):
        error_kernel(factor, patches, *refs)

    return pl.pallas_call(
        body,
        grid_spec=pltpu.PrefetchScalarGridSpec(
            num_scalar_prefetch=1,
            grid=(n,),
            in_specs=[pl.BlockSpec((rows_in, width), lambda k, x: (0, 0))] * n
            + [pl.BlockSpec((blocks, 1, rows, both), lambda k, x: (0, lax.rem(x[0] + n - k, n), 0, 0))],
            out_specs=pl.BlockSpec((keep, columns), lambda k, x: (0, 0)),
            scratch_shapes=[pltpu.VMEM((rows_in, columns), F32), pltpu.VMEM((keep, columns), F32)],
        ),
        out_shape=jax.ShapeDtypeStruct((keep, columns), BF),
        compiler_params=pltpu.CompilerParams(vmem_limit_bytes=56 * MB),
        cost_estimate=pl.CostEstimate(
            flops=2 * n * width * (rows_in + keep) * columns,
            bytes_accessed=2 * n * width * (rows_in + both),
            transcendentals=columns,
        ),
    )(x, *normed, panels)


def ring(size, step):
    return [(i, (i + step) % size) for i in range(size)]


def spread_to_all(values, axes, size):
    return lax.all_to_all(jnp.broadcast_to(values[None], (size, *values.shape)), axes, split_axis=0, concat_axis=0)


def shards(images, keep_index, teacher_weight, student_weight):
    patches, slice_width = images.shape[1:]
    keep_count = keep_index.shape[1]
    rows, columns = teacher_weight.shape
    image = images[0]

    teacher_next = 0.999 * teacher_weight + (1.0 - 0.999) * student_weight
    panel = jnp.concatenate([teacher_next, student_weight], axis=1).astype(BF)
    panels = lax.all_gather(panel, "yl", axis=0, tiled=True)
    panels, image = lax.optimization_barrier((panels, image))
    panels = lax.all_gather(panels, ("z", "c"), axis=0, tiled=True).reshape(Z * C, Y, rows, 2 * columns)

    other = lax.ppermute(image, "yh", ring(H, 1))
    pair = jnp.where(
        lax.axis_index("yh") == 0,
        jnp.concatenate([image, other], axis=1),
        jnp.concatenate([other, image], axis=1),
    )
    arrived = [lax.ppermute(pair, "x", ring(X, step)) for step in range(1, X)]

    floats = image.astype(F32)
    own_mean = jnp.mean(floats, axis=1)
    own_moment = jnp.sum(jnp.square(floats - own_mean[:, None]), axis=1)
    parts = spread_to_all(jnp.stack([own_mean, own_moment]), ("x", "yh"), X * H)
    centre = jnp.mean(parts[:, 0], axis=0)
    moment = jnp.sum(parts[:, 1], axis=0) + slice_width * jnp.sum(jnp.square(parts[:, 0] - centre), axis=0)
    scale = lax.rsqrt(moment / D + 1e-06)
    centre, scale = centre[:, None], scale[:, None]

    select = (keep_index[0][:, None] == lax.broadcasted_iota(jnp.int32, (keep_count, patches), 1)).astype(BF)

    normed = [normalise(pair, centre, scale, select)]
    pieces = normed[0][patches:].reshape(keep_count, Z * C, rows).transpose(1, 0, 2)
    pieces = lax.all_to_all(pieces, ("z", "c"), split_axis=0, concat_axis=0)
    pieces = pieces.reshape(Z * C * keep_count, rows).T
    pieces, arrived = lax.optimization_barrier((pieces, arrived))
    owned = spread_to_all(pieces, "x", X).reshape(Y * rows, Z * C * keep_count)

    normed += [normalise(chunk, centre, scale, select) for chunk in arrived]
    total_kept = keep_count * Y * Z * C
    error = make_error(normed, patches, lax.axis_index("x").reshape(1), panels, 1.0 / math.sqrt(total_kept))
    errors = lax.all_gather(error, ("z", "c"), axis=0, tiled=True)
    partial = jnp.dot(owned, errors, preferred_element_type=F32).astype(BF).reshape(Y, rows, columns)
    partial = lax.all_to_all(partial, "yl", split_axis=0, concat_axis=0)
    student_grad = jnp.sum(partial.astype(F32), axis=0)
    return (teacher_next, student_grad)


def solution(mesh):
    fine = Mesh(mesh.devices.reshape(Y, Z, C, X, H), ("yl", "z", "c", "x", "yh"))
    rows, cols = ("yl", "z", "c"), ("x", "yh")
    return jax.shard_map(
        shards,
        mesh=fine,
        in_specs=(P(rows, None, cols), P(rows, None), P(rows, cols), P(rows, cols)),
        out_specs=(P(rows, cols), P(rows, cols)),
        check_vma=False,
    )
```

```python
import math

import jax
import jax.numpy as jnp
from jax import lax
from jax.experimental import pallas as pl
from jax.experimental.pallas import tpu as pltpu
from jax.sharding import Mesh
from jax.sharding import PartitionSpec as P

D = 6144
Y, Z, C, X, H = 4, 8, 2, 4, 2
BF, F32 = jnp.bfloat16, jnp.float32
MB = 1024 * 1024
STREAMS = 4


def normalise_kernel(image_ref, centre_ref, scale_ref, select_ref, normed_ref):
    patches = image_ref.shape[0]
    normed = ((image_ref[...].astype(F32) - centre_ref[...]) * scale_ref[...]).astype(BF)
    normed_ref[:patches] = normed
    normed_ref[patches:] = jnp.dot(select_ref[...], normed, preferred_element_type=F32).astype(BF)


def normalise(chunk, centre, scale, select):
    patches, width = chunk.shape
    keep = select.shape[0]
    return pl.pallas_call(
        normalise_kernel,
        out_shape=jax.ShapeDtypeStruct((patches + keep, width), BF),
        compiler_params=pltpu.CompilerParams(vmem_limit_bytes=16 * MB),
        cost_estimate=pl.CostEstimate(
            flops=2 * keep * patches * width, bytes_accessed=2 * width * (2 * patches + keep), transcendentals=0
        ),
    )(chunk, centre, scale, select)


def error_kernel(factor, patches, x_ref, *refs):
    n = pl.num_programs(0)
    normed_refs, panel_refs = refs[:Y], refs[Y : Y + STREAMS]
    error_ref, teacher_acc, student_acc = refs[Y + STREAMS :]
    step = pl.program_id(0)
    columns = error_ref.shape[1]
    panel = jnp.concatenate([ref[:, 0].reshape(-1, 2 * columns) for ref in panel_refs], axis=0)
    for k in range(Y):

        @pl.when(step == k)
        def _(k=k):
            teacher = jnp.dot(normed_refs[k][...], panel[:, :columns], preferred_element_type=F32)
            student = jnp.dot(normed_refs[k][patches:], panel[:, columns:], preferred_element_type=F32)
            teacher_acc[...] = teacher if k == 0 else teacher_acc[...] + teacher
            student_acc[...] = student if k == 0 else student_acc[...] + student

    @pl.when(step == n - 1)
    def _():
        teacher = teacher_acc[:patches]
        centre = jnp.mean(teacher, axis=0, keepdims=True)
        centred = teacher - centre
        spread = jnp.mean(centred * centred, axis=0, keepdims=True)
        target = (teacher_acc[patches:] - centre) * lax.rsqrt(spread + 1e-05)
        error_ref[...] = ((student_acc[...] - target) * factor).astype(BF)


def make_error(normed, patches, x, panels, factor):
    n = len(normed)
    rows_in, width = normed[0].shape
    keep = rows_in - patches
    blocks, _, rows, both = panels.shape
    columns = both // 2

    def body(*refs):
        error_kernel(factor, patches, *refs)

    return pl.pallas_call(
        body,
        grid_spec=pltpu.PrefetchScalarGridSpec(
            num_scalar_prefetch=1,
            grid=(n,),
            in_specs=[pl.BlockSpec((rows_in, width), lambda k, x: (0, 0))] * n
            + [
                pl.BlockSpec((blocks // STREAMS, 1, rows, both), lambda k, x, i=i: (i, lax.rem(x[0] + n - k, n), 0, 0))
                for i in range(STREAMS)
            ],
            out_specs=pl.BlockSpec((keep, columns), lambda k, x: (0, 0)),
            scratch_shapes=[pltpu.VMEM((rows_in, columns), F32), pltpu.VMEM((keep, columns), F32)],
        ),
        out_shape=jax.ShapeDtypeStruct((keep, columns), BF),
        compiler_params=pltpu.CompilerParams(vmem_limit_bytes=56 * MB),
        cost_estimate=pl.CostEstimate(
            flops=2 * n * width * (rows_in + keep) * columns,
            bytes_accessed=2 * n * width * (rows_in + both),
            transcendentals=columns,
        ),
    )(x, *normed, *[panels] * STREAMS)


def ring(size, step):
    return [(i, (i + step) % size) for i in range(size)]


def spread_to_all(values, axes, size):
    return lax.all_to_all(jnp.broadcast_to(values[None], (size, *values.shape)), axes, split_axis=0, concat_axis=0)


def shards(images, keep_index, teacher_weight, student_weight):
    patches, slice_width = images.shape[1:]
    keep_count = keep_index.shape[1]
    rows, columns = teacher_weight.shape
    image = images[0]

    teacher_next = 0.999 * teacher_weight + (1.0 - 0.999) * student_weight
    panel = jnp.concatenate([teacher_next, student_weight], axis=1).astype(BF)
    panels = lax.all_gather(panel, "yl", axis=0, tiled=True)
    panels, image = lax.optimization_barrier((panels, image))
    panels = lax.all_gather(panels, ("z", "c"), axis=0, tiled=True).reshape(Z * C, Y, rows, 2 * columns)

    other = lax.ppermute(image, "yh", ring(H, 1))
    pair = jnp.where(
        lax.axis_index("yh") == 0,
        jnp.concatenate([image, other], axis=1),
        jnp.concatenate([other, image], axis=1),
    )
    arrived = [lax.ppermute(pair, "x", ring(X, step)) for step in range(1, X)]

    floats = image.astype(F32)
    own_mean = jnp.mean(floats, axis=1)
    own_moment = jnp.sum(jnp.square(floats - own_mean[:, None]), axis=1)
    parts = spread_to_all(jnp.stack([own_mean, own_moment]), ("x", "yh"), X * H)
    centre = jnp.mean(parts[:, 0], axis=0)
    moment = jnp.sum(parts[:, 1], axis=0) + slice_width * jnp.sum(jnp.square(parts[:, 0] - centre), axis=0)
    scale = lax.rsqrt(moment / D + 1e-06)
    centre, scale = centre[:, None], scale[:, None]

    select = (keep_index[0][:, None] == lax.broadcasted_iota(jnp.int32, (keep_count, patches), 1)).astype(BF)

    normed = [normalise(pair, centre, scale, select)]
    pieces = normed[0][patches:].reshape(keep_count, Z * C, rows).transpose(1, 0, 2)
    pieces = lax.all_to_all(pieces, ("z", "c"), split_axis=0, concat_axis=0)
    pieces = pieces.reshape(Z * C * keep_count, rows).T
    pieces, arrived = lax.optimization_barrier((pieces, arrived))
    owned = spread_to_all(pieces, "x", X).reshape(Y * rows, Z * C * keep_count)

    normed += [normalise(chunk, centre, scale, select) for chunk in arrived]
    normed, owned = lax.optimization_barrier((normed, owned))
    total_kept = keep_count * Y * Z * C
    error = make_error(normed, patches, lax.axis_index("x").reshape(1), panels, 1.0 / math.sqrt(total_kept))
    errors = lax.all_gather(error, ("z", "c"), axis=0, tiled=True)
    partial = jnp.dot(owned, errors, preferred_element_type=F32).astype(BF).reshape(Y, rows, columns)
    partial = lax.all_to_all(partial, "yl", split_axis=0, concat_axis=0)
    student_grad = jnp.sum(partial.astype(F32), axis=0)
    return (teacher_next, student_grad)


def solution(mesh):
    fine = Mesh(mesh.devices.reshape(Y, Z, C, X, H), ("yl", "z", "c", "x", "yh"))
    rows, cols = ("yl", "z", "c"), ("x", "yh")
    return jax.shard_map(
        shards,
        mesh=fine,
        in_specs=(P(rows, None, cols), P(rows, None), P(rows, cols), P(rows, cols)),
        out_specs=(P(rows, cols), P(rows, cols)),
        check_vma=False,
    )
```

```python
import math

import jax
import jax.numpy as jnp
from jax import lax
from jax.experimental import pallas as pl
from jax.experimental.pallas import tpu as pltpu
from jax.sharding import Mesh
from jax.sharding import PartitionSpec as P

D = 6144
Y, Z, C, X, H = 4, 8, 2, 4, 2
BF, F32 = jnp.bfloat16, jnp.float32
MB = 1024 * 1024
PARTS = 1


def normalised(chunk_ref, centre_ref, scale_ref):
    return ((chunk_ref[...].astype(F32) - centre_ref[...]) * scale_ref[...]).astype(BF)


def kept(select_ref, normed):
    return jnp.dot(select_ref[...], normed, preferred_element_type=F32).astype(BF)


def pick_kernel(chunk_ref, centre_ref, scale_ref, select_ref, picked_ref):
    picked_ref[...] = kept(select_ref, normalised(chunk_ref, centre_ref, scale_ref))


def pick(chunk, centre, scale, select):
    patches, width = chunk.shape
    keep = select.shape[0]
    return pl.pallas_call(
        pick_kernel,
        out_shape=jax.ShapeDtypeStruct((keep, width), BF),
        compiler_params=pltpu.CompilerParams(vmem_limit_bytes=16 * MB),
        cost_estimate=pl.CostEstimate(
            flops=2 * keep * patches * width, bytes_accessed=2 * width * (patches + keep), transcendentals=0
        ),
    )(chunk, centre, scale, select)


def normalise_kernel(*refs):
    chunk_refs, (centre_ref, scale_ref, select_ref, normed_ref) = refs[:-4], refs[-4:]
    patches = centre_ref.shape[0]
    for k, chunk_ref in enumerate(chunk_refs):

        @pl.when(pl.program_id(0) == k)
        def _(chunk_ref=chunk_ref):
            normed = normalised(chunk_ref, centre_ref, scale_ref)
            normed_ref[0, :patches] = normed
            normed_ref[0, patches:] = kept(select_ref, normed)


def normalise(chunks, centre, scale, select):
    n = len(chunks)
    patches, width = chunks[0].shape
    keep = select.shape[0]
    whole = lambda k: (0, 0)
    return pl.pallas_call(
        normalise_kernel,
        grid=(n,),
        in_specs=[pl.BlockSpec((patches, width), whole)] * n
        + [pl.BlockSpec((patches, 1), whole)] * 2
        + [pl.BlockSpec((keep, patches), whole)],
        out_specs=pl.BlockSpec((1, patches + keep, width), lambda k: (k, 0, 0)),
        out_shape=jax.ShapeDtypeStruct((n, patches + keep, width), BF),
        compiler_params=pltpu.CompilerParams(vmem_limit_bytes=32 * MB),
        cost_estimate=pl.CostEstimate(
            flops=2 * n * keep * patches * width, bytes_accessed=2 * n * width * (2 * patches + keep), transcendentals=0
        ),
    )(*chunks, centre, scale, select)


def error_kernel(factor, patches, x_ref, normed_ref, panel_ref, error_ref, teacher_acc, student_acc):
    step = pl.program_id(0)
    columns = error_ref.shape[1]
    panel = panel_ref[:, 0].reshape(-1, 2 * columns)
    teacher_part = jnp.dot(normed_ref[0], panel[:, :columns], preferred_element_type=F32)
    student_part = jnp.dot(normed_ref[0, patches:], panel[:, columns:], preferred_element_type=F32)

    @pl.when(step == 0)
    def _():
        teacher_acc[...] = teacher_part
        student_acc[...] = student_part

    @pl.when(step > 0)
    def _():
        teacher_acc[...] += teacher_part
        student_acc[...] += student_part

    @pl.when(step == pl.num_programs(0) - 1)
    def _():
        teacher = teacher_acc[:patches]
        centre = jnp.mean(teacher, axis=0, keepdims=True)
        centred = teacher - centre
        spread = jnp.mean(centred * centred, axis=0, keepdims=True)
        target = (teacher_acc[patches:] - centre) * lax.rsqrt(spread + 1e-05)
        error_ref[...] = ((student_acc[...] - target) * factor).astype(BF)


def make_error(normed, patches, x, panels, factor):
    n, rows_in, width = normed.shape
    keep = rows_in - patches
    blocks, _, rows, both = panels.shape
    columns = both // 2

    def body(*refs):
        error_kernel(factor, patches, *refs)

    return pl.pallas_call(
        body,
        grid_spec=pltpu.PrefetchScalarGridSpec(
            num_scalar_prefetch=1,
            grid=(n * PARTS,),
            in_specs=[
                pl.BlockSpec((1, rows_in, width // PARTS), lambda k, x: (k // PARTS, 0, lax.rem(k, PARTS))),
                pl.BlockSpec(
                    (blocks // PARTS, 1, rows, both),
                    lambda k, x: (lax.rem(k, PARTS), lax.rem(x[0] + n - k // PARTS, n), 0, 0),
                ),
            ],
            out_specs=pl.BlockSpec((keep, columns), lambda k, x: (0, 0)),
            scratch_shapes=[pltpu.VMEM((rows_in, columns), F32), pltpu.VMEM((keep, columns), F32)],
        ),
        out_shape=jax.ShapeDtypeStruct((keep, columns), BF),
        compiler_params=pltpu.CompilerParams(vmem_limit_bytes=56 * MB),
        cost_estimate=pl.CostEstimate(
            flops=2 * n * width * (rows_in + keep) * columns,
            bytes_accessed=2 * n * width * (rows_in + both),
            transcendentals=columns,
        ),
    )(x, normed, panels)


def ring(size, step):
    return [(i, (i + step) % size) for i in range(size)]


def spread_to_all(values, axes, size):
    return lax.all_to_all(jnp.broadcast_to(values[None], (size, *values.shape)), axes, split_axis=0, concat_axis=0)


def shards(images, keep_index, teacher_weight, student_weight):
    patches, slice_width = images.shape[1:]
    keep_count = keep_index.shape[1]
    rows, columns = teacher_weight.shape
    image = images[0]

    teacher_next = 0.999 * teacher_weight + (1.0 - 0.999) * student_weight
    panel = jnp.concatenate([teacher_next, student_weight], axis=1).astype(BF)
    panels = lax.all_gather(panel, "yl", axis=0, tiled=True)
    panels, image = lax.optimization_barrier((panels, image))
    panels = lax.all_gather(panels, ("z", "c"), axis=0, tiled=True).reshape(Z * C, Y, rows, 2 * columns)

    other = lax.ppermute(image, "yh", ring(H, 1))
    pair = jnp.where(
        lax.axis_index("yh") == 0,
        jnp.concatenate([image, other], axis=1),
        jnp.concatenate([other, image], axis=1),
    )
    arrived = [lax.ppermute(pair, "x", ring(X, step)) for step in range(1, X)]

    floats = image.astype(F32)
    own_mean = jnp.mean(floats, axis=1)
    own_moment = jnp.sum(jnp.square(floats - own_mean[:, None]), axis=1)
    parts = spread_to_all(jnp.stack([own_mean, own_moment]), ("x", "yh"), X * H)
    centre = jnp.mean(parts[:, 0], axis=0)
    moment = jnp.sum(parts[:, 1], axis=0) + slice_width * jnp.sum(jnp.square(parts[:, 0] - centre), axis=0)
    scale = lax.rsqrt(moment / D + 1e-06)
    centre, scale = centre[:, None], scale[:, None]

    select = (keep_index[0][:, None] == lax.broadcasted_iota(jnp.int32, (keep_count, patches), 1)).astype(BF)

    pieces = pick(pair, centre, scale, select).reshape(keep_count, Z * C, rows).transpose(1, 0, 2)
    pieces = lax.all_to_all(pieces, ("z", "c"), split_axis=0, concat_axis=0)
    pieces = pieces.reshape(Z * C * keep_count, rows).T
    pieces, arrived = lax.optimization_barrier((pieces, arrived))
    owned = spread_to_all(pieces, "x", X).reshape(Y * rows, Z * C * keep_count)

    normed = normalise([pair, *arrived], centre, scale, select)
    total_kept = keep_count * Y * Z * C
    error = make_error(normed, patches, lax.axis_index("x").reshape(1), panels, 1.0 / math.sqrt(total_kept))
    errors = lax.all_gather(error, ("z", "c"), axis=0, tiled=True)
    partial = jnp.dot(owned, errors, preferred_element_type=F32).astype(BF).reshape(Y, rows, columns)
    partial = lax.all_to_all(partial, "yl", split_axis=0, concat_axis=0)
    student_grad = jnp.sum(partial.astype(F32), axis=0)
    return (teacher_next, student_grad)


def solution(mesh):
    fine = Mesh(mesh.devices.reshape(Y, Z, C, X, H), ("yl", "z", "c", "x", "yh"))
    rows, cols = ("yl", "z", "c"), ("x", "yh")
    return jax.shard_map(
        shards,
        mesh=fine,
        in_specs=(P(rows, None, cols), P(rows, None), P(rows, cols), P(rows, cols)),
        out_specs=(P(rows, cols), P(rows, cols)),
        check_vma=False,
    )
```

```python
import math

import jax
import jax.numpy as jnp
from jax import lax
from jax.experimental import pallas as pl
from jax.experimental.pallas import tpu as pltpu
from jax.sharding import Mesh
from jax.sharding import PartitionSpec as P

D = 6144
Y, Z, C, X, H = 4, 8, 2, 4, 2
BF, F32 = jnp.bfloat16, jnp.float32
MB = 1024 * 1024


def normalise_kernel(rows, x_ref, *refs):
    count = (len(refs) - 6)
    chunk_refs, (centre_ref, scale_ref, select_ref, normed_ref, pieces_ref, picked_ref) = refs[:count], refs[count:]
    patches = centre_ref.shape[0]
    step = pl.program_id(0)
    for k, chunk_ref in enumerate(chunk_refs):

        @pl.when(lax.rem(x_ref[0] + count - step, count) == k)
        def _(chunk_ref=chunk_ref):
            normed = ((chunk_ref[...].astype(F32) - centre_ref[...]) * scale_ref[...]).astype(BF)
            picked = jnp.dot(select_ref[...], normed, preferred_element_type=F32)
            normed_ref[0, :patches] = normed
            normed_ref[0, patches:] = picked.astype(BF)
            picked_ref[...] = picked

    for i in range(count):

        @pl.when(step == i)
        def _(i=i):
            for piece in range(pieces_ref.shape[0]):
                pieces_ref[piece, :, i * rows : (i + 1) * rows] = picked_ref[:, piece * rows : (piece + 1) * rows].astype(BF)


def normalise(chunks, x, centre, scale, select, rows):
    n = len(chunks)
    patches, width = chunks[0].shape
    keep = select.shape[0]
    whole = lambda k, x: (0, 0)

    def body(*refs):
        normalise_kernel(rows, *refs)

    return pl.pallas_call(
        body,
        grid_spec=pltpu.PrefetchScalarGridSpec(
            num_scalar_prefetch=1,
            grid=(n,),
            in_specs=[pl.BlockSpec((patches, width), whole)] * n
            + [pl.BlockSpec((patches, 1), whole)] * 2
            + [pl.BlockSpec((keep, patches), whole)],
            out_specs=[
                pl.BlockSpec((1, patches + keep, width), lambda k, x: (k, 0, 0)),
                pl.BlockSpec((width // rows, keep, n * rows), lambda k, x: (0, 0, 0)),
            ],
            scratch_shapes=[pltpu.VMEM((keep, width), F32)],
        ),
        out_shape=[
            jax.ShapeDtypeStruct((n, patches + keep, width), BF),
            jax.ShapeDtypeStruct((width // rows, keep, n * rows), BF),
        ],
        compiler_params=pltpu.CompilerParams(vmem_limit_bytes=32 * MB),
        cost_estimate=pl.CostEstimate(
            flops=2 * n * keep * patches * width, bytes_accessed=4 * n * width * (patches + keep), transcendentals=0
        ),
    )(x, *chunks, centre, scale, select)


def error_kernel(factor, patches, normed_ref, panel_ref, error_ref, teacher_acc, student_acc):
    step = pl.program_id(0)
    columns = error_ref.shape[1]
    panel = panel_ref[:, 0].reshape(-1, 2 * columns)
    teacher_part = jnp.dot(normed_ref[0], panel[:, :columns], preferred_element_type=F32)
    student_part = jnp.dot(normed_ref[0, patches:], panel[:, columns:], preferred_element_type=F32)

    @pl.when(step == 0)
    def _():
        teacher_acc[...] = teacher_part
        student_acc[...] = student_part

    @pl.when(step > 0)
    def _():
        teacher_acc[...] += teacher_part
        student_acc[...] += student_part

    @pl.when(step == pl.num_programs(0) - 1)
    def _():
        teacher = teacher_acc[:patches]
        centre = jnp.mean(teacher, axis=0, keepdims=True)
        centred = teacher - centre
        spread = jnp.mean(centred * centred, axis=0, keepdims=True)
        target = (teacher_acc[patches:] - centre) * lax.rsqrt(spread + 1e-05)
        error_ref[...] = ((student_acc[...] - target) * factor).astype(BF)


def make_error(normed, patches, panels, factor):
    n, rows_in, width = normed.shape
    keep = rows_in - patches
    blocks, _, rows, both = panels.shape
    columns = both // 2

    def body(*refs):
        error_kernel(factor, patches, *refs)

    return pl.pallas_call(
        body,
        grid=(n,),
        in_specs=[
            pl.BlockSpec((1, rows_in, width), lambda k: (k, 0, 0)),
            pl.BlockSpec((blocks, 1, rows, both), lambda k: (0, k, 0, 0)),
        ],
        out_specs=pl.BlockSpec((keep, columns), lambda k: (0, 0)),
        out_shape=jax.ShapeDtypeStruct((keep, columns), BF),
        scratch_shapes=[pltpu.VMEM((rows_in, columns), F32), pltpu.VMEM((keep, columns), F32)],
        compiler_params=pltpu.CompilerParams(vmem_limit_bytes=56 * MB),
        cost_estimate=pl.CostEstimate(
            flops=2 * n * width * (rows_in + keep) * columns,
            bytes_accessed=2 * n * width * (rows_in + both),
            transcendentals=columns,
        ),
    )(normed, panels)


def ring(size, step):
    return [(i, (i + step) % size) for i in range(size)]


def spread_to_all(values, axes, size):
    return lax.all_to_all(jnp.broadcast_to(values[None], (size, *values.shape)), axes, split_axis=0, concat_axis=0)


def shards(images, keep_index, teacher_weight, student_weight):
    patches, slice_width = images.shape[1:]
    keep_count = keep_index.shape[1]
    rows, columns = teacher_weight.shape
    image = images[0]

    teacher_next = 0.999 * teacher_weight + (1.0 - 0.999) * student_weight
    panel = jnp.concatenate([teacher_next, student_weight], axis=1).astype(BF)
    panels = lax.all_gather(panel, "yl", axis=0, tiled=True)
    panels, image = lax.optimization_barrier((panels, image))
    panels = lax.all_gather(panels, ("z", "c"), axis=0, tiled=True).reshape(Z * C, Y, rows, 2 * columns)

    other = lax.ppermute(image, "yh", ring(H, 1))
    pair = jnp.where(
        lax.axis_index("yh") == 0,
        jnp.concatenate([image, other], axis=1),
        jnp.concatenate([other, image], axis=1),
    )
    arrived = [lax.ppermute(pair, "x", ring(X, step)) for step in range(1, X)]

    floats = image.astype(F32)
    own_mean = jnp.mean(floats, axis=1)
    own_moment = jnp.sum(jnp.square(floats - own_mean[:, None]), axis=1)
    parts = spread_to_all(jnp.stack([own_mean, own_moment]), ("x", "yh"), X * H)
    centre = jnp.mean(parts[:, 0], axis=0)
    moment = jnp.sum(parts[:, 1], axis=0) + slice_width * jnp.sum(jnp.square(parts[:, 0] - centre), axis=0)
    scale = lax.rsqrt(moment / D + 1e-06)
    centre, scale = centre[:, None], scale[:, None]

    select = (keep_index[0][:, None] == lax.broadcasted_iota(jnp.int32, (keep_count, patches), 1)).astype(BF)

    x = lax.axis_index("x").reshape(1)
    normed, pieces = normalise([pair, *arrived], x, centre, scale, select, rows)
    owned = lax.all_to_all(pieces, ("z", "c"), split_axis=0, concat_axis=0).reshape(Z * C * keep_count, Y * rows)

    total_kept = keep_count * Y * Z * C
    error = make_error(normed, patches, panels, 1.0 / math.sqrt(total_kept))
    errors = lax.all_gather(error, ("z", "c"), axis=0, tiled=True)
    partial = lax.dot_general(owned, errors, (((0,), (0,)), ((), ())), preferred_element_type=F32)
    partial = partial.astype(BF).reshape(Y, rows, columns)
    partial = lax.all_to_all(partial, "yl", split_axis=0, concat_axis=0)
    student_grad = jnp.sum(partial.astype(F32), axis=0)
    return (teacher_next, student_grad)


def solution(mesh):
    fine = Mesh(mesh.devices.reshape(Y, Z, C, X, H), ("yl", "z", "c", "x", "yh"))
    rows, cols = ("yl", "z", "c"), ("x", "yh")
    return jax.shard_map(
        shards,
        mesh=fine,
        in_specs=(P(rows, None, cols), P(rows, None), P(rows, cols), P(rows, cols)),
        out_specs=(P(rows, cols), P(rows, cols)),
        check_vma=False,
    )
```

```python
import math

import jax
import jax.numpy as jnp
from jax import lax
from jax.experimental import pallas as pl
from jax.experimental.pallas import tpu as pltpu
from jax.sharding import Mesh
from jax.sharding import PartitionSpec as P

D = 6144
Y, Z, C, X, H = 4, 8, 2, 4, 2
BF, F32 = jnp.bfloat16, jnp.float32
MB = 1024 * 1024
PARTS = 1


def normalised(chunk_ref, centre_ref, scale_ref):
    return ((chunk_ref[...].astype(F32) - centre_ref[...]) * scale_ref[...]).astype(BF)


def kept(select_ref, normed):
    return jnp.dot(select_ref[...], normed, preferred_element_type=F32).astype(BF)


def pick_kernel(chunk_ref, centre_ref, scale_ref, select_ref, picked_ref):
    picked_ref[...] = kept(select_ref, normalised(chunk_ref, centre_ref, scale_ref))


def pick(chunk, centre, scale, select):
    patches, width = chunk.shape
    keep = select.shape[0]
    return pl.pallas_call(
        pick_kernel,
        out_shape=jax.ShapeDtypeStruct((keep, width), BF),
        compiler_params=pltpu.CompilerParams(vmem_limit_bytes=16 * MB),
        cost_estimate=pl.CostEstimate(
            flops=2 * keep * patches * width, bytes_accessed=2 * width * (patches + keep), transcendentals=0
        ),
    )(chunk, centre, scale, select)


def normalise_kernel(*refs):
    chunk_refs, (centre_ref, scale_ref, select_ref, normed_ref) = refs[:-4], refs[-4:]
    patches = centre_ref.shape[0]
    for k, chunk_ref in enumerate(chunk_refs):

        @pl.when(pl.program_id(0) == k)
        def _(chunk_ref=chunk_ref):
            normed = normalised(chunk_ref, centre_ref, scale_ref)
            normed_ref[0, :patches] = normed
            normed_ref[0, patches:] = kept(select_ref, normed)


def normalise(chunks, centre, scale, select):
    n = len(chunks)
    patches, width = chunks[0].shape
    keep = select.shape[0]
    whole = lambda k: (0, 0)
    return pl.pallas_call(
        normalise_kernel,
        grid=(n,),
        in_specs=[pl.BlockSpec((patches, width), whole)] * n
        + [pl.BlockSpec((patches, 1), whole)] * 2
        + [pl.BlockSpec((keep, patches), whole)],
        out_specs=pl.BlockSpec((1, patches + keep, width), lambda k: (k, 0, 0)),
        out_shape=jax.ShapeDtypeStruct((n, patches + keep, width), BF),
        compiler_params=pltpu.CompilerParams(vmem_limit_bytes=32 * MB),
        cost_estimate=pl.CostEstimate(
            flops=2 * n * keep * patches * width, bytes_accessed=2 * n * width * (2 * patches + keep), transcendentals=0
        ),
    )(*chunks, centre, scale, select)


def error_kernel(factor, patches, x_ref, normed_ref, panel_ref, error_ref, teacher_acc, student_acc):
    step = pl.program_id(0)
    columns = error_ref.shape[1]
    panel = panel_ref[:, 0].reshape(-1, 2 * columns)
    teacher_part = jnp.dot(normed_ref[0], panel[:, :columns], preferred_element_type=F32)
    student_part = jnp.dot(normed_ref[0, patches:], panel[:, columns:], preferred_element_type=F32)

    @pl.when(step == 0)
    def _():
        teacher_acc[...] = teacher_part
        student_acc[...] = student_part

    @pl.when(step > 0)
    def _():
        teacher_acc[...] += teacher_part
        student_acc[...] += student_part

    @pl.when(step == pl.num_programs(0) - 1)
    def _():
        teacher = teacher_acc[:patches]
        centre = jnp.mean(teacher, axis=0, keepdims=True)
        centred = teacher - centre
        spread = jnp.mean(centred * centred, axis=0, keepdims=True)
        target = (teacher_acc[patches:] - centre) * lax.rsqrt(spread + 1e-05)
        error_ref[...] = ((student_acc[...] - target) * factor).astype(BF)


def make_error(normed, patches, x, panels, factor):
    n, rows_in, width = normed.shape
    keep = rows_in - patches
    blocks, _, rows, both = panels.shape
    columns = both // 2

    def body(*refs):
        error_kernel(factor, patches, *refs)

    return pl.pallas_call(
        body,
        grid_spec=pltpu.PrefetchScalarGridSpec(
            num_scalar_prefetch=1,
            grid=(n * PARTS,),
            in_specs=[
                pl.BlockSpec((1, rows_in, width // PARTS), lambda k, x: (k // PARTS, 0, lax.rem(k, PARTS))),
                pl.BlockSpec(
                    (blocks // PARTS, 1, rows, both),
                    lambda k, x: (lax.rem(k, PARTS), lax.rem(x[0] + n - k // PARTS, n), 0, 0),
                ),
            ],
            out_specs=pl.BlockSpec((keep, columns), lambda k, x: (0, 0)),
            scratch_shapes=[pltpu.VMEM((rows_in, columns), F32), pltpu.VMEM((keep, columns), F32)],
        ),
        out_shape=jax.ShapeDtypeStruct((keep, columns), BF),
        compiler_params=pltpu.CompilerParams(vmem_limit_bytes=56 * MB),
        cost_estimate=pl.CostEstimate(
            flops=2 * n * width * (rows_in + keep) * columns,
            bytes_accessed=2 * n * width * (rows_in + both),
            transcendentals=columns,
        ),
    )(x, normed, panels)


def ring(size, step):
    return [(i, (i + step) % size) for i in range(size)]


def spread_to_all(values, axes, size):
    return lax.all_to_all(jnp.broadcast_to(values[None], (size, *values.shape)), axes, split_axis=0, concat_axis=0)


def shards(images, keep_index, teacher_weight, student_weight):
    patches, slice_width = images.shape[1:]
    keep_count = keep_index.shape[1]
    rows, columns = teacher_weight.shape
    image = images[0]

    teacher_next = 0.999 * teacher_weight + (1.0 - 0.999) * student_weight
    panel = jnp.concatenate([teacher_next, student_weight], axis=1).astype(BF)
    panels = lax.all_gather(panel, "yl", axis=0, tiled=True)
    panels, image = lax.optimization_barrier((panels, image))
    panels = lax.all_gather(panels, ("z", "c"), axis=0, tiled=True).reshape(Z * C, Y, rows, 2 * columns)

    other = lax.ppermute(image, "yh", ring(H, 1))
    pair = jnp.where(
        lax.axis_index("yh") == 0,
        jnp.concatenate([image, other], axis=1),
        jnp.concatenate([other, image], axis=1),
    )
    arrived = [lax.ppermute(pair, "x", ring(X, step)) for step in range(1, X)]

    floats = image.astype(F32)
    own_mean = jnp.mean(floats, axis=1)
    own_moment = jnp.sum(jnp.square(floats - own_mean[:, None]), axis=1)
    parts = spread_to_all(jnp.stack([own_mean, own_moment]), ("x", "yh"), X * H)
    centre = jnp.mean(parts[:, 0], axis=0)
    moment = jnp.sum(parts[:, 1], axis=0) + slice_width * jnp.sum(jnp.square(parts[:, 0] - centre), axis=0)
    scale = lax.rsqrt(moment / D + 1e-06)
    centre, scale = centre[:, None], scale[:, None]

    select = (keep_index[0][:, None] == lax.broadcasted_iota(jnp.int32, (keep_count, patches), 1)).astype(BF)

    pieces = pick(pair, centre, scale, select).reshape(keep_count, Z * C, rows).transpose(1, 0, 2)
    pieces = lax.all_to_all(pieces, ("z", "c"), split_axis=0, concat_axis=0)
    pieces = pieces.reshape(Z * C * keep_count, rows).T
    pieces, arrived = lax.optimization_barrier((pieces, arrived))
    normed = normalise([pair, *arrived], centre, scale, select)
    pieces, normed = lax.optimization_barrier((pieces, normed))
    owned = spread_to_all(pieces, "x", X).reshape(Y * rows, Z * C * keep_count)

    total_kept = keep_count * Y * Z * C
    error = make_error(normed, patches, lax.axis_index("x").reshape(1), panels, 1.0 / math.sqrt(total_kept))
    errors = lax.all_gather(error, ("z", "c"), axis=0, tiled=True)
    partial = jnp.dot(owned, errors, preferred_element_type=F32).astype(BF).reshape(Y, rows, columns)
    partial = lax.all_to_all(partial, "yl", split_axis=0, concat_axis=0)
    student_grad = jnp.sum(partial.astype(F32), axis=0)
    return (teacher_next, student_grad)


def solution(mesh):
    fine = Mesh(mesh.devices.reshape(Y, Z, C, X, H), ("yl", "z", "c", "x", "yh"))
    rows, cols = ("yl", "z", "c"), ("x", "yh")
    return jax.shard_map(
        shards,
        mesh=fine,
        in_specs=(P(rows, None, cols), P(rows, None), P(rows, cols), P(rows, cols)),
        out_specs=(P(rows, cols), P(rows, cols)),
        check_vma=False,
    )
```

```python
import math

import jax
import jax.numpy as jnp
from jax import lax
from jax.experimental import pallas as pl
from jax.experimental.pallas import tpu as pltpu
from jax.sharding import Mesh
from jax.sharding import PartitionSpec as P

D = 6144
Y, Z, C, X, H = 4, 8, 2, 4, 2
BF, F32 = jnp.bfloat16, jnp.float32
MB = 1024 * 1024
PARTS = 1


def normalised(chunk_ref, centre_ref, scale_ref):
    return ((chunk_ref[...].astype(F32) - centre_ref[...]) * scale_ref[...]).astype(BF)


def kept(select_ref, normed):
    return jnp.dot(select_ref[...], normed, preferred_element_type=F32).astype(BF)


def pick_kernel(chunk_ref, centre_ref, scale_ref, select_ref, picked_ref):
    picked_ref[...] = kept(select_ref, normalised(chunk_ref, centre_ref, scale_ref))


def pick(chunk, centre, scale, select):
    patches, width = chunk.shape
    keep = select.shape[0]
    return pl.pallas_call(
        pick_kernel,
        out_shape=jax.ShapeDtypeStruct((keep, width), BF),
        compiler_params=pltpu.CompilerParams(vmem_limit_bytes=16 * MB),
        cost_estimate=pl.CostEstimate(
            flops=2 * keep * patches * width, bytes_accessed=2 * width * (patches + keep), transcendentals=0
        ),
    )(chunk, centre, scale, select)


def normalise_kernel(*refs):
    chunk_refs, (centre_ref, scale_ref, select_ref, normed_ref) = refs[:-4], refs[-4:]
    patches = centre_ref.shape[0]
    for k, chunk_ref in enumerate(chunk_refs):

        @pl.when(pl.program_id(0) == k)
        def _(chunk_ref=chunk_ref):
            normed = normalised(chunk_ref, centre_ref, scale_ref)
            normed_ref[0, :patches] = normed
            normed_ref[0, patches:] = kept(select_ref, normed)


def normalise(chunks, centre, scale, select):
    n = len(chunks)
    patches, width = chunks[0].shape
    keep = select.shape[0]
    whole = lambda k: (0, 0)
    return pl.pallas_call(
        normalise_kernel,
        grid=(n,),
        in_specs=[pl.BlockSpec((patches, width), whole)] * n
        + [pl.BlockSpec((patches, 1), whole)] * 2
        + [pl.BlockSpec((keep, patches), whole)],
        out_specs=pl.BlockSpec((1, patches + keep, width), lambda k: (k, 0, 0)),
        out_shape=jax.ShapeDtypeStruct((n, patches + keep, width), BF),
        compiler_params=pltpu.CompilerParams(vmem_limit_bytes=32 * MB),
        cost_estimate=pl.CostEstimate(
            flops=2 * n * keep * patches * width, bytes_accessed=2 * n * width * (2 * patches + keep), transcendentals=0
        ),
    )(*chunks, centre, scale, select)


def turn_kernel(rows_ref, copies_ref):
    turned = rows_ref[...].reshape(-1, rows_ref.shape[-1]).T
    for k in range(copies_ref.shape[0]):
        copies_ref[k] = turned


def turned_copies(values, count):
    width = values.shape[-1]
    return pl.pallas_call(
        turn_kernel,
        out_shape=jax.ShapeDtypeStruct((count, width, values.size // width), values.dtype),
        compiler_params=pltpu.CompilerParams(vmem_limit_bytes=16 * MB),
        cost_estimate=pl.CostEstimate(flops=0, bytes_accessed=2 * (count + 1) * values.size, transcendentals=0),
    )(values)


def error_kernel(factor, patches, x_ref, normed_ref, panel_ref, error_ref, teacher_acc, student_acc):
    step = pl.program_id(0)
    columns = error_ref.shape[1]
    panel = panel_ref[:, 0].reshape(-1, 2 * columns)
    teacher_part = jnp.dot(normed_ref[0], panel[:, :columns], preferred_element_type=F32)
    student_part = jnp.dot(normed_ref[0, patches:], panel[:, columns:], preferred_element_type=F32)

    @pl.when(step == 0)
    def _():
        teacher_acc[...] = teacher_part
        student_acc[...] = student_part

    @pl.when(step > 0)
    def _():
        teacher_acc[...] += teacher_part
        student_acc[...] += student_part

    @pl.when(step == pl.num_programs(0) - 1)
    def _():
        teacher = teacher_acc[:patches]
        centre = jnp.mean(teacher, axis=0, keepdims=True)
        centred = teacher - centre
        spread = jnp.mean(centred * centred, axis=0, keepdims=True)
        target = (teacher_acc[patches:] - centre) * lax.rsqrt(spread + 1e-05)
        error_ref[...] = ((student_acc[...] - target) * factor).astype(BF)


def make_error(normed, patches, x, panels, factor):
    n, rows_in, width = normed.shape
    keep = rows_in - patches
    blocks, _, rows, both = panels.shape
    columns = both // 2

    def body(*refs):
        error_kernel(factor, patches, *refs)

    return pl.pallas_call(
        body,
        grid_spec=pltpu.PrefetchScalarGridSpec(
            num_scalar_prefetch=1,
            grid=(n * PARTS,),
            in_specs=[
                pl.BlockSpec((1, rows_in, width // PARTS), lambda k, x: (k // PARTS, 0, lax.rem(k, PARTS))),
                pl.BlockSpec(
                    (blocks // PARTS, 1, rows, both),
                    lambda k, x: (lax.rem(k, PARTS), lax.rem(x[0] + n - k // PARTS, n), 0, 0),
                ),
            ],
            out_specs=pl.BlockSpec((keep, columns), lambda k, x: (0, 0)),
            scratch_shapes=[pltpu.VMEM((rows_in, columns), F32), pltpu.VMEM((keep, columns), F32)],
        ),
        out_shape=jax.ShapeDtypeStruct((keep, columns), BF),
        compiler_params=pltpu.CompilerParams(vmem_limit_bytes=56 * MB),
        cost_estimate=pl.CostEstimate(
            flops=2 * n * width * (rows_in + keep) * columns,
            bytes_accessed=2 * n * width * (rows_in + both),
            transcendentals=columns,
        ),
    )(x, normed, panels)


def ring(size, step):
    return [(i, (i + step) % size) for i in range(size)]


def spread_to_all(values, axes, size):
    return lax.all_to_all(jnp.broadcast_to(values[None], (size, *values.shape)), axes, split_axis=0, concat_axis=0)


def shards(images, keep_index, teacher_weight, student_weight):
    patches, slice_width = images.shape[1:]
    keep_count = keep_index.shape[1]
    rows, columns = teacher_weight.shape
    image = images[0]

    teacher_next = 0.999 * teacher_weight + (1.0 - 0.999) * student_weight
    panel = jnp.concatenate([teacher_next, student_weight], axis=1).astype(BF)
    panels = lax.all_gather(panel, "yl", axis=0, tiled=True)
    panels, image = lax.optimization_barrier((panels, image))
    panels = lax.all_gather(panels, ("z", "c"), axis=0, tiled=True).reshape(Z * C, Y, rows, 2 * columns)

    other = lax.ppermute(image, "yh", ring(H, 1))
    pair = jnp.where(
        lax.axis_index("yh") == 0,
        jnp.concatenate([image, other], axis=1),
        jnp.concatenate([other, image], axis=1),
    )
    arrived = [lax.ppermute(pair, "x", ring(X, step)) for step in range(1, X)]

    floats = image.astype(F32)
    own_mean = jnp.mean(floats, axis=1)
    own_moment = jnp.sum(jnp.square(floats - own_mean[:, None]), axis=1)
    parts = spread_to_all(jnp.stack([own_mean, own_moment]), ("x", "yh"), X * H)
    centre = jnp.mean(parts[:, 0], axis=0)
    moment = jnp.sum(parts[:, 1], axis=0) + slice_width * jnp.sum(jnp.square(parts[:, 0] - centre), axis=0)
    scale = lax.rsqrt(moment / D + 1e-06)
    centre, scale = centre[:, None], scale[:, None]

    select = (keep_index[0][:, None] == lax.broadcasted_iota(jnp.int32, (keep_count, patches), 1)).astype(BF)

    pieces = pick(pair, centre, scale, select).reshape(keep_count, Z * C, rows).transpose(1, 0, 2)
    pieces = lax.all_to_all(pieces, ("z", "c"), split_axis=0, concat_axis=0)
    copies = turned_copies(pieces, X)
    pieces, arrived = lax.optimization_barrier((pieces, arrived))
    normed = normalise([pair, *arrived], centre, scale, select)
    copies, _ = lax.optimization_barrier((copies, normed))
    owned = lax.all_to_all(copies, "x", split_axis=0, concat_axis=0).reshape(Y * rows, Z * C * keep_count)

    total_kept = keep_count * Y * Z * C
    error = make_error(normed, patches, lax.axis_index("x").reshape(1), panels, 1.0 / math.sqrt(total_kept))
    errors = lax.all_gather(error, ("z", "c"), axis=0, tiled=True)
    partial = jnp.dot(owned, errors, preferred_element_type=F32).astype(BF).reshape(Y, rows, columns)
    partial = lax.all_to_all(partial, "yl", split_axis=0, concat_axis=0)
    student_grad = jnp.sum(partial.astype(F32), axis=0)
    return (teacher_next, student_grad)


def solution(mesh):
    fine = Mesh(mesh.devices.reshape(Y, Z, C, X, H), ("yl", "z", "c", "x", "yh"))
    rows, cols = ("yl", "z", "c"), ("x", "yh")
    return jax.shard_map(
        shards,
        mesh=fine,
        in_specs=(P(rows, None, cols), P(rows, None), P(rows, cols), P(rows, cols)),
        out_specs=(P(rows, cols), P(rows, cols)),
        check_vma=False,
    )
```

```python
import math

import jax
import jax.numpy as jnp
from jax import lax
from jax.experimental import pallas as pl
from jax.experimental.pallas import tpu as pltpu
from jax.sharding import Mesh
from jax.sharding import PartitionSpec as P

D = 6144
Y, Z, C, X, H = 4, 8, 2, 4, 2
BF, F32 = jnp.bfloat16, jnp.float32
MB = 1024 * 1024
PARTS = 1


def normalised(chunk_ref, centre_ref, scale_ref):
    return ((chunk_ref[...].astype(F32) - centre_ref[...]) * scale_ref[...]).astype(BF)


def kept(select_ref, normed):
    return jnp.dot(select_ref[...], normed, preferred_element_type=F32).astype(BF)


def pick_kernel(chunk_ref, centre_ref, scale_ref, select_ref, pieces_ref, picked_ref):
    normed = normalised(chunk_ref, centre_ref, scale_ref)
    picked_ref[...] = jnp.dot(select_ref[...], normed, preferred_element_type=F32)
    count, _, rows = pieces_ref.shape
    for piece in range(count):
        pieces_ref[piece] = picked_ref[:, piece * rows : (piece + 1) * rows].astype(BF)


def pick(chunk, centre, scale, select, rows):
    patches, width = chunk.shape
    keep = select.shape[0]
    return pl.pallas_call(
        pick_kernel,
        out_shape=jax.ShapeDtypeStruct((width // rows, keep, rows), BF),
        scratch_shapes=[pltpu.VMEM((keep, width), F32)],
        compiler_params=pltpu.CompilerParams(vmem_limit_bytes=16 * MB),
        cost_estimate=pl.CostEstimate(
            flops=2 * keep * patches * width, bytes_accessed=2 * width * (patches + keep), transcendentals=0
        ),
    )(chunk, centre, scale, select)


def normalise_kernel(*refs):
    chunk_refs, (centre_ref, scale_ref, select_ref, normed_ref) = refs[:-4], refs[-4:]
    patches = centre_ref.shape[0]
    for k, chunk_ref in enumerate(chunk_refs):

        @pl.when(pl.program_id(0) == k)
        def _(chunk_ref=chunk_ref):
            normed = normalised(chunk_ref, centre_ref, scale_ref)
            normed_ref[0, :patches] = normed
            normed_ref[0, patches:] = kept(select_ref, normed)


def normalise(chunks, centre, scale, select):
    n = len(chunks)
    patches, width = chunks[0].shape
    keep = select.shape[0]
    whole = lambda k: (0, 0)
    return pl.pallas_call(
        normalise_kernel,
        grid=(n,),
        in_specs=[pl.BlockSpec((patches, width), whole)] * n
        + [pl.BlockSpec((patches, 1), whole)] * 2
        + [pl.BlockSpec((keep, patches), whole)],
        out_specs=pl.BlockSpec((1, patches + keep, width), lambda k: (k, 0, 0)),
        out_shape=jax.ShapeDtypeStruct((n, patches + keep, width), BF),
        compiler_params=pltpu.CompilerParams(vmem_limit_bytes=32 * MB),
        cost_estimate=pl.CostEstimate(
            flops=2 * n * keep * patches * width, bytes_accessed=2 * n * width * (2 * patches + keep), transcendentals=0
        ),
    )(*chunks, centre, scale, select)


def turn_kernel(rows_ref, copies_ref):
    turned = rows_ref[...].reshape(-1, rows_ref.shape[-1]).T
    for k in range(copies_ref.shape[0]):
        copies_ref[k] = turned


def turned_copies(values, count):
    width = values.shape[-1]
    return pl.pallas_call(
        turn_kernel,
        out_shape=jax.ShapeDtypeStruct((count, width, values.size // width), values.dtype),
        compiler_params=pltpu.CompilerParams(vmem_limit_bytes=16 * MB),
        cost_estimate=pl.CostEstimate(flops=0, bytes_accessed=2 * (count + 1) * values.size, transcendentals=0),
    )(values)


def error_kernel(factor, patches, x_ref, normed_ref, panel_ref, error_ref, teacher_acc, student_acc):
    step = pl.program_id(0)
    columns = error_ref.shape[1]
    panel = panel_ref[:, 0].reshape(-1, 2 * columns)
    teacher_part = jnp.dot(normed_ref[0], panel[:, :columns], preferred_element_type=F32)
    student_part = jnp.dot(normed_ref[0, patches:], panel[:, columns:], preferred_element_type=F32)

    @pl.when(step == 0)
    def _():
        teacher_acc[...] = teacher_part
        student_acc[...] = student_part

    @pl.when(step > 0)
    def _():
        teacher_acc[...] += teacher_part
        student_acc[...] += student_part

    @pl.when(step == pl.num_programs(0) - 1)
    def _():
        teacher = teacher_acc[:patches]
        centre = jnp.mean(teacher, axis=0, keepdims=True)
        centred = teacher - centre
        spread = jnp.mean(centred * centred, axis=0, keepdims=True)
        target = (teacher_acc[patches:] - centre) * lax.rsqrt(spread + 1e-05)
        error_ref[...] = ((student_acc[...] - target) * factor).astype(BF)


def make_error(normed, patches, x, panels, factor):
    n, rows_in, width = normed.shape
    keep = rows_in - patches
    blocks, _, rows, both = panels.shape
    columns = both // 2

    def body(*refs):
        error_kernel(factor, patches, *refs)

    return pl.pallas_call(
        body,
        grid_spec=pltpu.PrefetchScalarGridSpec(
            num_scalar_prefetch=1,
            grid=(n * PARTS,),
            in_specs=[
                pl.BlockSpec((1, rows_in, width // PARTS), lambda k, x: (k // PARTS, 0, lax.rem(k, PARTS))),
                pl.BlockSpec(
                    (blocks // PARTS, 1, rows, both),
                    lambda k, x: (lax.rem(k, PARTS), lax.rem(x[0] + n - k // PARTS, n), 0, 0),
                ),
            ],
            out_specs=pl.BlockSpec((keep, columns), lambda k, x: (0, 0)),
            scratch_shapes=[pltpu.VMEM((rows_in, columns), F32), pltpu.VMEM((keep, columns), F32)],
        ),
        out_shape=jax.ShapeDtypeStruct((keep, columns), BF),
        compiler_params=pltpu.CompilerParams(vmem_limit_bytes=56 * MB),
        cost_estimate=pl.CostEstimate(
            flops=2 * n * width * (rows_in + keep) * columns,
            bytes_accessed=2 * n * width * (rows_in + both),
            transcendentals=columns,
        ),
    )(x, normed, panels)


def ring(size, step):
    return [(i, (i + step) % size) for i in range(size)]


def spread_to_all(values, axes, size):
    return lax.all_to_all(jnp.broadcast_to(values[None], (size, *values.shape)), axes, split_axis=0, concat_axis=0)


def shards(images, keep_index, teacher_weight, student_weight):
    patches, slice_width = images.shape[1:]
    keep_count = keep_index.shape[1]
    rows, columns = teacher_weight.shape
    image = images[0]

    teacher_next = 0.999 * teacher_weight + (1.0 - 0.999) * student_weight
    panel = jnp.concatenate([teacher_next, student_weight], axis=1).astype(BF)
    panels = lax.all_gather(panel, "yl", axis=0, tiled=True)
    panels, image = lax.optimization_barrier((panels, image))
    panels = lax.all_gather(panels, ("z", "c"), axis=0, tiled=True).reshape(Z * C, Y, rows, 2 * columns)

    other = lax.ppermute(image, "yh", ring(H, 1))
    pair = jnp.where(
        lax.axis_index("yh") == 0,
        jnp.concatenate([image, other], axis=1),
        jnp.concatenate([other, image], axis=1),
    )
    arrived = [lax.ppermute(pair, "x", ring(X, step)) for step in range(1, X)]

    floats = image.astype(F32)
    own_mean = jnp.mean(floats, axis=1)
    own_moment = jnp.sum(jnp.square(floats - own_mean[:, None]), axis=1)
    parts = spread_to_all(jnp.stack([own_mean, own_moment]), ("x", "yh"), X * H)
    centre = jnp.mean(parts[:, 0], axis=0)
    moment = jnp.sum(parts[:, 1], axis=0) + slice_width * jnp.sum(jnp.square(parts[:, 0] - centre), axis=0)
    scale = lax.rsqrt(moment / D + 1e-06)
    centre, scale = centre[:, None], scale[:, None]

    select = (keep_index[0][:, None] == lax.broadcasted_iota(jnp.int32, (keep_count, patches), 1)).astype(BF)

    pieces = pick(pair, centre, scale, select, rows)
    pieces = lax.all_to_all(pieces, ("z", "c"), split_axis=0, concat_axis=0)
    copies = turned_copies(pieces, X)
    pieces, arrived = lax.optimization_barrier((pieces, arrived))
    normed = normalise([pair, *arrived], centre, scale, select)
    copies, _ = lax.optimization_barrier((copies, normed))
    owned = lax.all_to_all(copies, "x", split_axis=0, concat_axis=0).reshape(Y * rows, Z * C * keep_count)

    total_kept = keep_count * Y * Z * C
    error = make_error(normed, patches, lax.axis_index("x").reshape(1), panels, 1.0 / math.sqrt(total_kept))
    errors = lax.all_gather(error, ("z", "c"), axis=0, tiled=True)
    partial = jnp.dot(owned, errors, preferred_element_type=F32).astype(BF).reshape(Y, rows, columns)
    partial = lax.all_to_all(partial, "yl", split_axis=0, concat_axis=0)
    student_grad = jnp.sum(partial.astype(F32), axis=0)
    return (teacher_next, student_grad)


def solution(mesh):
    fine = Mesh(mesh.devices.reshape(Y, Z, C, X, H), ("yl", "z", "c", "x", "yh"))
    rows, cols = ("yl", "z", "c"), ("x", "yh")
    return jax.shard_map(
        shards,
        mesh=fine,
        in_specs=(P(rows, None, cols), P(rows, None), P(rows, cols), P(rows, cols)),
        out_specs=(P(rows, cols), P(rows, cols)),
        check_vma=False,
    )
```

```python
import math

import jax
import jax.numpy as jnp
from jax import lax
from jax.experimental import pallas as pl
from jax.experimental.pallas import tpu as pltpu
from jax.sharding import Mesh
from jax.sharding import PartitionSpec as P

D = 6144
Y, Z, C, X, H = 4, 8, 2, 4, 2
BF, F32 = jnp.bfloat16, jnp.float32
MB = 1024 * 1024


def normalised(chunk_ref, centre_ref, scale_ref):
    return ((chunk_ref[...].astype(F32) - centre_ref[...]) * scale_ref[...]).astype(BF)


def kept(select_ref, normed):
    return jnp.dot(select_ref[...], normed, preferred_element_type=F32).astype(BF)


def pick_kernel(chunk_ref, centre_ref, scale_ref, select_ref, pieces_ref, picked_ref):
    normed = normalised(chunk_ref, centre_ref, scale_ref)
    picked_ref[...] = jnp.dot(select_ref[...], normed, preferred_element_type=F32)
    count, _, rows = pieces_ref.shape
    for piece in range(count):
        pieces_ref[piece] = picked_ref[:, piece * rows : (piece + 1) * rows].astype(BF)


def pick(chunk, centre, scale, select, rows):
    patches, width = chunk.shape
    keep = select.shape[0]
    return pl.pallas_call(
        pick_kernel,
        out_shape=jax.ShapeDtypeStruct((width // rows, keep, rows), BF),
        scratch_shapes=[pltpu.VMEM((keep, width), F32)],
        compiler_params=pltpu.CompilerParams(vmem_limit_bytes=16 * MB),
        cost_estimate=pl.CostEstimate(
            flops=2 * keep * patches * width, bytes_accessed=2 * width * (patches + keep), transcendentals=0
        ),
    )(chunk, centre, scale, select)


def normalise_kernel(*refs):
    chunk_refs, (centre_ref, scale_ref, select_ref, normed_ref) = refs[:-4], refs[-4:]
    patches = centre_ref.shape[0]
    for k, chunk_ref in enumerate(chunk_refs):

        @pl.when(pl.program_id(0) == k)
        def _(chunk_ref=chunk_ref):
            normed = normalised(chunk_ref, centre_ref, scale_ref)
            normed_ref[0, :patches] = normed
            normed_ref[0, patches:] = kept(select_ref, normed)


def normalise(chunks, centre, scale, select):
    n = len(chunks)
    patches, width = chunks[0].shape
    keep = select.shape[0]
    whole = lambda k: (0, 0)
    return pl.pallas_call(
        normalise_kernel,
        grid=(n,),
        in_specs=[pl.BlockSpec((patches, width), whole)] * n
        + [pl.BlockSpec((patches, 1), whole)] * 2
        + [pl.BlockSpec((keep, patches), whole)],
        out_specs=pl.BlockSpec((1, patches + keep, width), lambda k: (k, 0, 0)),
        out_shape=jax.ShapeDtypeStruct((n, patches + keep, width), BF),
        compiler_params=pltpu.CompilerParams(vmem_limit_bytes=32 * MB),
        cost_estimate=pl.CostEstimate(
            flops=2 * n * keep * patches * width, bytes_accessed=2 * n * width * (2 * patches + keep), transcendentals=0
        ),
    )(*chunks, centre, scale, select)


def turn_kernel(rows_ref, copies_ref):
    turned = rows_ref[...].reshape(-1, rows_ref.shape[-1]).T
    for k in range(copies_ref.shape[0]):
        copies_ref[k] = turned


def turned_copies(values, count):
    width = values.shape[-1]
    return pl.pallas_call(
        turn_kernel,
        out_shape=jax.ShapeDtypeStruct((count, width, values.size // width), values.dtype),
        compiler_params=pltpu.CompilerParams(vmem_limit_bytes=16 * MB),
        cost_estimate=pl.CostEstimate(flops=0, bytes_accessed=2 * (count + 1) * values.size, transcendentals=0),
    )(values)


def error_kernel(factor, patches, x_ref, normed_ref, near_ref, far_ref, error_ref, teacher_acc, student_acc):
    step = pl.program_id(0)
    columns = error_ref.shape[1]
    panel = jnp.concatenate([ref[:, 0].reshape(-1, 2 * columns) for ref in (near_ref, far_ref)], axis=0)
    teacher_part = jnp.dot(normed_ref[0], panel[:, :columns], preferred_element_type=F32)
    student_part = jnp.dot(normed_ref[0, patches:], panel[:, columns:], preferred_element_type=F32)

    @pl.when(step == 0)
    def _():
        teacher_acc[...] = teacher_part
        student_acc[...] = student_part

    @pl.when(step > 0)
    def _():
        teacher_acc[...] += teacher_part
        student_acc[...] += student_part

    @pl.when(step == pl.num_programs(0) - 1)
    def _():
        teacher = teacher_acc[:patches]
        centre = jnp.mean(teacher, axis=0, keepdims=True)
        centred = teacher - centre
        spread = jnp.mean(centred * centred, axis=0, keepdims=True)
        target = (teacher_acc[patches:] - centre) * lax.rsqrt(spread + 1e-05)
        error_ref[...] = ((student_acc[...] - target) * factor).astype(BF)


def make_error(normed, patches, x, panels, factor):
    n, rows_in, width = normed.shape
    keep = rows_in - patches
    blocks, _, rows, both = panels.shape
    columns = both // 2

    def body(*refs):
        error_kernel(factor, patches, *refs)

    return pl.pallas_call(
        body,
        grid_spec=pltpu.PrefetchScalarGridSpec(
            num_scalar_prefetch=1,
            grid=(n,),
            in_specs=[
                pl.BlockSpec((1, rows_in, width), lambda k, x: (k, 0, 0)),
            ]
            + [
                pl.BlockSpec((blocks // 2, 1, rows, both), lambda k, x, i=i: (i, lax.rem(x[0] + n - k, n), 0, 0))
                for i in range(2)
            ],
            out_specs=pl.BlockSpec((keep, columns), lambda k, x: (0, 0)),
            scratch_shapes=[pltpu.VMEM((rows_in, columns), F32), pltpu.VMEM((keep, columns), F32)],
        ),
        out_shape=jax.ShapeDtypeStruct((keep, columns), BF),
        compiler_params=pltpu.CompilerParams(vmem_limit_bytes=56 * MB),
        cost_estimate=pl.CostEstimate(
            flops=2 * n * width * (rows_in + keep) * columns,
            bytes_accessed=2 * n * width * (rows_in + both),
            transcendentals=columns,
        ),
    )(x, normed, panels, panels)


def ring(size, step):
    return [(i, (i + step) % size) for i in range(size)]


def spread_to_all(values, axes, size):
    return lax.all_to_all(jnp.broadcast_to(values[None], (size, *values.shape)), axes, split_axis=0, concat_axis=0)


def shards(images, keep_index, teacher_weight, student_weight):
    patches, slice_width = images.shape[1:]
    keep_count = keep_index.shape[1]
    rows, columns = teacher_weight.shape
    image = images[0]

    teacher_next = 0.999 * teacher_weight + (1.0 - 0.999) * student_weight
    panel = jnp.concatenate([teacher_next, student_weight], axis=1).astype(BF)
    panels = lax.all_gather(panel, "yl", axis=0, tiled=True)
    panels, image = lax.optimization_barrier((panels, image))
    panels = lax.all_gather(panels, ("z", "c"), axis=0, tiled=True).reshape(Z * C, Y, rows, 2 * columns)

    other = lax.ppermute(image, "yh", ring(H, 1))
    pair = jnp.where(
        lax.axis_index("yh") == 0,
        jnp.concatenate([image, other], axis=1),
        jnp.concatenate([other, image], axis=1),
    )
    arrived = [lax.ppermute(pair, "x", ring(X, step)) for step in range(1, X)]

    floats = image.astype(F32)
    own_mean = jnp.mean(floats, axis=1)
    own_moment = jnp.sum(jnp.square(floats - own_mean[:, None]), axis=1)
    parts = spread_to_all(jnp.stack([own_mean, own_moment]), ("x", "yh"), X * H)
    centre = jnp.mean(parts[:, 0], axis=0)
    moment = jnp.sum(parts[:, 1], axis=0) + slice_width * jnp.sum(jnp.square(parts[:, 0] - centre), axis=0)
    scale = lax.rsqrt(moment / D + 1e-06)
    centre, scale = centre[:, None], scale[:, None]

    select = (keep_index[0][:, None] == lax.broadcasted_iota(jnp.int32, (keep_count, patches), 1)).astype(BF)

    pieces = pick(pair, centre, scale, select, rows)
    pieces = lax.all_to_all(pieces, ("z", "c"), split_axis=0, concat_axis=0)
    copies = turned_copies(pieces, X)
    pieces, arrived = lax.optimization_barrier((pieces, arrived))
    normed = normalise([pair, *arrived], centre, scale, select)
    copies, _ = lax.optimization_barrier((copies, normed))
    owned = lax.all_to_all(copies, "x", split_axis=0, concat_axis=0).reshape(Y * rows, Z * C * keep_count)

    total_kept = keep_count * Y * Z * C
    error = make_error(normed, patches, lax.axis_index("x").reshape(1), panels, 1.0 / math.sqrt(total_kept))
    errors = lax.all_gather(error, ("z", "c"), axis=0, tiled=True)
    partial = jnp.dot(owned, errors, preferred_element_type=F32).astype(BF).reshape(Y, rows, columns)
    partial = lax.all_to_all(partial, "yl", split_axis=0, concat_axis=0)
    student_grad = jnp.sum(partial.astype(F32), axis=0)
    return (teacher_next, student_grad)


def solution(mesh):
    fine = Mesh(mesh.devices.reshape(Y, Z, C, X, H), ("yl", "z", "c", "x", "yh"))
    rows, cols = ("yl", "z", "c"), ("x", "yh")
    return jax.shard_map(
        shards,
        mesh=fine,
        in_specs=(P(rows, None, cols), P(rows, None), P(rows, cols), P(rows, cols)),
        out_specs=(P(rows, cols), P(rows, cols)),
        check_vma=False,
    )
```
